32 devices in a mesh: gx: 8 (over y, x, core), gy: 4 (over z).
Axes of the slice: x: 2, y: 2, z: 4, core: 2. Of those that a mesh axis runs over, the one named last changes fastest.
Arguments:
- tokens: bfloat16 [256, 16384], P('gy', 'gx'), may hold values from -6 to 6
- gate_weight: bfloat16 [16384, 26624], P('gx', 'gy'), may hold values from -0.046875 to 0.046875
- up_weight: bfloat16 [16384, 26624], P('gx', 'gy'), may hold values from -0.046875 to 0.046875
- down_weight: bfloat16 [26624, 16384], P('gy', 'gx'), may hold values from -0.0390625 to 0.0390625
Outputs:
- layer_out: bfloat16 [256, 16384], P('gy', 'gx')
The draws below stay inside these ranges and needn't reach their ends.
All inputs are finite; a program needn't handle non-finite values.
Results may differ from the reference program's by a relative error of at most 0.0049.
Values may be sent and summed in bfloat16 or wider, within the bound.
No kernel may reach another device: no remote copies, remote signals or barrier semaphores. Data moves between devices by JAX's collectives and lax.ppermute only.
A program may use at most 192 MiB of HBM per device.

```python
import jax
import jax.numpy as jnp

D = 16384
HID = 26624
TOKENS = 256


def levels(stream_key, shape, split, low, largest):
    loudness = 1.0
    for position, parts in split:
        steps = jax.random.uniform(jax.random.fold_in(jax.random.fold_in(stream_key, 6), position), (parts,), jnp.float32, low / len(split), largest / len(split))
        loudness = loudness * jnp.repeat(jnp.exp(steps), shape[position] // parts).reshape((-1,) + (1,) * (len(shape) - 1 - position))
    return loudness


def scatter_about(key, dims, scale, most, pieces=(), dtype=jnp.bfloat16):
    values = jax.random.normal(key, dims, jnp.float32) * scale
    if len(pieces) > 0:
        values = levels(key, dims, pieces, -0.22, 0.18) * values
    return jnp.clip(values, min=-most, max=most).astype(dtype)


def setup_inputs(seed: int = 0) -> dict:
    key_of = jax.random.split(jax.random.key(seed), 5)
    return {
        "tokens": scatter_about(key_of[0], (TOKENS, D), 1.0, 6.0, ((0, 4), (1, 8))),
        "gate_weight": scatter_about(key_of[1], (D, HID), D ** -0.5, 0.046875, ((0, 8), (1, 4))),
        "up_weight": scatter_about(key_of[2], (D, HID), D ** -0.5, 0.046875, ((0, 8), (1, 4))),
        "down_weight": scatter_about(key_of[3], (HID, D), HID ** -0.5, 0.0390625, ((0, 4), (1, 8))),
    }


def reference(tokens, gate_weight, up_weight, down_weight):
    gate = jnp.dot(tokens, gate_weight, preferred_element_type=jnp.float32)
    up = jnp.dot(tokens, up_weight, preferred_element_type=jnp.float32)
    hidden = (jax.nn.silu(gate) * up).astype(jnp.bfloat16)
    return jnp.dot(hidden, down_weight, preferred_element_type=jnp.float32).astype(jnp.bfloat16)
```

```python
import jax
import jax.numpy as jnp
from jax import lax
from jax.experimental import pallas as pl
from jax.experimental.pallas import tpu as pltpu
from jax.sharding import PartitionSpec as P

F32 = jnp.float32
BF16 = jnp.bfloat16
PIECES = (4, 4, 5)
HELD = ((0, 0), (0, 1), (1, 0), (1, 1))


def params(mib):
    return pltpu.CompilerParams(vmem_limit_bytes=mib << 20)


def cost(m, k, n):
    return pl.CostEstimate(flops=2 * m * k * n, transcendentals=0, bytes_accessed=2 * (m * k + k * n) + 4 * m * n)


def widths(units):
    total, ends, run = sum(PIECES), [0], 0
    for piece in PIECES:
        run += piece
        ends.append(round(units * run / total))
    return [(a, b) for a, b in zip(ends, ends[1:]) if b > a]


def block_of(size):
    return next(b for b in (512, 256, 128) if size % b == 0)


def row_blocks(groups):
    chips = groups // 2
    return [(h, 2 * q + core) for core in range(2) for h in range(2) for q in range(chips)]


def place_rows(me, parts, groups):
    rows = sum(p.shape[0] for p in parts)
    cols = parts[0].shape[1]
    step = rows // (2 * groups)

    def kernel(me_ref, *refs):
        ins, out, buf = refs[:-2], refs[-2], refs[-1]
        at = 0
        for r in ins:
            buf[at : at + r.shape[0], :] = r[...]
            at += r.shape[0]
        for i, (h, p) in enumerate(row_blocks(groups)):
            src = pl.multiple_of((h * groups + (me_ref[0] ^ p)) * step, step)
            out[i * step : (i + 1) * step, :] = buf[pl.ds(src, step), :]

    whole = lambda a: pl.BlockSpec(a.shape, lambda i, m: (0, 0))
    return pl.pallas_call(
        kernel,
        grid_spec=pltpu.PrefetchScalarGridSpec(
            num_scalar_prefetch=1,
            grid=(1,),
            in_specs=[whole(p) for p in parts],
            out_specs=pl.BlockSpec((rows, cols), lambda i, m: (0, 0)),
            scratch_shapes=[pltpu.VMEM((rows, cols), BF16)],
        ),
        out_shape=jax.ShapeDtypeStruct((rows, cols), BF16),
        compiler_params=params(4),
    )(me, *parts)


def fetch(weights, chunks, bn):
    k = weights[0].shape[0]
    shapes = [pltpu.VMEM((k, (last - first) * bn), BF16) for _, first, last in chunks]
    count = len(chunks)

    def kernel(*refs):
        ins, outs, sems = refs[: len(weights)], refs[len(weights) : -1], refs[-1]
        copies = []
        for i, (which, first, last) in enumerate(chunks):
            cols = pl.ds(first * bn, (last - first) * bn)
            copies.append(pltpu.make_async_copy(ins[which].at[:, cols], outs[i], sems.at[i]))
        for c in copies:
            c.start()
        for c in copies:
            c.wait()

    return pl.pallas_call(
        kernel,
        in_specs=[pl.BlockSpec(memory_space=pl.ANY)] * len(weights),
        out_specs=[pl.BlockSpec(memory_space=pltpu.VMEM)] * count,
        out_shape=shapes,
        scratch_shapes=[pltpu.SemaphoreType.DMA((count,))],
        compiler_params=params(1),
        cost_estimate=pl.CostEstimate(flops=0, transcendentals=0, bytes_accessed=4 * weights[0].size),
    )(*weights)


def gate_up(feats, pair, held, first, last, bn):
    rows, k = feats.shape
    half, n = rows // 2, last - first

    def kernel(x, g, u, keep, send):
        cols = pl.ds(pl.multiple_of(pl.program_id(0) * bn, bn), bn)
        for i, w in enumerate((g, u)):
            tile = w[:, cols] if held[i] else w[...]
            part = jnp.dot(x[...], tile, preferred_element_type=F32)
            keep[i] = part[:half]
            send[i] = part[half:].astype(BF16)

    o_spec = pl.BlockSpec((2, half, bn), lambda j: (0, 0, j))
    stream = pl.BlockSpec((k, bn), lambda j: (0, first + j))
    return pl.pallas_call(
        kernel,
        grid=(n,),
        in_specs=[pl.BlockSpec((rows, k), lambda j: (0, 0))]
        + [pl.BlockSpec(memory_space=pltpu.VMEM) if h else stream for h in held],
        out_specs=[o_spec, o_spec],
        out_shape=[
            jax.ShapeDtypeStruct((2, half, n * bn), F32),
            jax.ShapeDtypeStruct((2, half, n * bn), BF16),
        ],
        compiler_params=params(5 if all(held) else 45),
        cost_estimate=cost(rows, k, 2 * n * bn),
    )(feats, *pair)


def down(me, hiddens, acc, down_weight, start, groups, owners):
    w = hiddens[0].shape[1]
    rows, n = sum(h.shape[0] for h in hiddens), down_weight.shape[1]
    step = rows // (2 * groups)
    bn = block_of(n)
    count = len(hiddens)

    def kernel(me_ref, *refs):
        refs = list(refs)
        ins, wd = refs[:count], refs[count]
        prev = refs[count + 1] if acc is not None else None
        outs, lhs = refs[count + 1 + (acc is not None) : -1], refs[-1]

        @pl.when(pl.program_id(0) == 0)
        def _():
            per = len(row_blocks(groups)) // count
            for i, (h, p) in enumerate(row_blocks(groups)):
                at = (i % per) * step
                dst = pl.multiple_of((h * groups + (me_ref[0] ^ p)) * step, step)
                lhs[pl.ds(dst, step), :] = ins[i // per][at : at + step, :]

        total = jnp.dot(lhs[...], wd[...], preferred_element_type=F32)
        if prev is not None:
            total = total + prev[...]
        each = rows // len(outs)
        for s, o in enumerate(outs):
            o[...] = total[s * each : (s + 1) * each].astype(o.dtype)

    in_specs = [pl.BlockSpec(h.shape, lambda j, m: (0, 0)) for h in hiddens]
    in_specs.append(pl.BlockSpec((pl.Element(w), pl.Element(bn)), lambda j, m: (start, j * bn)))
    args = [*hiddens, down_weight]
    if acc is not None:
        in_specs.append(pl.BlockSpec((rows, bn), lambda j, m: (0, j)))
        args.append(acc)
    each = rows // owners
    out_shape = [jax.ShapeDtypeStruct((each, n), F32 if s == 0 else BF16) for s in range(owners)]
    return pl.pallas_call(
        kernel,
        grid_spec=pltpu.PrefetchScalarGridSpec(
            num_scalar_prefetch=1,
            grid=(n // bn,),
            in_specs=in_specs,
            out_specs=[pl.BlockSpec((each, bn), lambda j, m: (0, j))] * owners,
            scratch_shapes=[pltpu.VMEM((rows, w), BF16)],
        ),
        out_shape=out_shape,
        compiler_params=params(40),
        cost_estimate=cost(rows, w, n),
    )(me, *args)


def make(nx, nz):
    def swap(v, mask):
        return lax.ppermute(v, "gx", [(i, i ^ mask) for i in range(nx)])

    def shift(v, s):
        return lax.ppermute(v, "gy", [(i, (i + s) % nz) for i in range(nz)])

    chips = nx // 2
    bits = chips.bit_length() - 1

    def layer(tokens, gate_weight, up_weight, down_weight):
        me = lax.axis_index("gx").astype(jnp.int32).reshape(1)
        parts = [tokens] + [shift(tokens, s) for s in range(1, nz)]
        feats = place_rows(me, parts, nx)
        hid = gate_weight.shape[1]
        bn = block_of(hid)
        chunks = widths(hid // bn)
        both = (gate_weight, up_weight)
        early = [(i, *chunks[c]) for c, i in HELD]
        got = fetch(both, early, bn)
        weights = [list(both) for _ in chunks]
        for (c, i), v in zip(HELD, got):
            weights[c][i] = v
        own = feats.shape[0] // (2 * nx)
        acc = None
        for c, (first, last) in enumerate(chunks):
            keep, send = gate_up(feats, weights[c], [(c, i) in HELD for i in range(2)], first, last, bn)
            got = swap(send, 1)
            halves = []
            for h in range(2):
                order = range(bits) if h == 0 else range(bits)[::-1]
                rows = slice(h * chips * own, (h + 1) * chips * own)
                block = keep[:, rows] + got[:, rows].astype(F32)
                for i, b in enumerate(order):
                    wide = block.reshape(2, -1, 2, block.shape[1] // 2 ** (1 + sum(1 for o in order[i + 1 :] if o > b)), block.shape[2])
                    stay, go = wide[:, :, 0], wide[:, :, 1].astype(BF16)
                    flat = (2, block.shape[1] // 2, block.shape[2])
                    come = swap(go.reshape(flat), 2 << b)
                    block = stay.reshape(flat) + come.astype(F32)
                hidden = (jax.nn.silu(block[0]) * block[1]).astype(BF16)
                for i, b in reversed(list(enumerate(order))):
                    come = swap(hidden, 2 << b)
                    inner = own * 2 ** sum(1 for o in order[i + 1 :] if o < b)
                    both = [v.reshape(-1, 1, inner, v.shape[1]) for v in (hidden, come)]
                    hidden = jnp.concatenate(both, axis=1).reshape(-1, hidden.shape[1])
                halves.append(hidden)
            halves += [swap(v, 1) for v in halves]
            final = c == len(chunks) - 1
            acc = down(me, halves, acc, down_weight, first * bn, nx, nz if final else 1)
            acc = acc if final else acc[0]
        out = acc[0]
        for s in range(1, nz):
            out = out + shift(acc[s], -s).astype(F32)
        return out.astype(BF16)

    return layer


def solution(mesh):
    return jax.shard_map(
        make(mesh.shape["gx"], mesh.shape["gy"]),
        mesh=mesh,
        in_specs=(P("gy", "gx"), P("gx", "gy"), P("gx", "gy"), P("gy", "gx")),
        out_specs=P("gy", "gx"),
        check_vma=False,
    )
```

```python
import jax
import jax.numpy as jnp
from jax import lax
from jax.experimental import pallas as pl
from jax.experimental.pallas import tpu as pltpu
from jax.sharding import PartitionSpec as P

F32 = jnp.float32
BF16 = jnp.bfloat16
PIECES = (4, 5, 4)
GROUPS = (((0, 1, 2),), ((0,), (1, 2)))
HELD = ((0, 0), (0, 1), (1, 0), (1, 1))


def params(mib):
    return pltpu.CompilerParams(vmem_limit_bytes=mib << 20)


def cost(m, k, n):
    return pl.CostEstimate(flops=2 * m * k * n, transcendentals=0, bytes_accessed=2 * (m * k + k * n) + 4 * m * n)


def widths(units):
    total, ends, run = sum(PIECES), [0], 0
    for piece in PIECES:
        run += piece
        ends.append(round(units * run / total))
    return [(a, b) for a, b in zip(ends, ends[1:]) if b > a]


def block_of(size):
    return next(b for b in (512, 256, 128) if size % b == 0)


def row_blocks(groups):
    chips = groups // 2
    return [(h, 2 * q + core) for core in range(2) for h in range(2) for q in range(chips)]


def place_rows(me, parts, groups):
    rows = sum(p.shape[0] for p in parts)
    cols = parts[0].shape[1]
    step = rows // (2 * groups)

    def kernel(me_ref, *refs):
        ins, out, buf = refs[:-2], refs[-2], refs[-1]
        at = 0
        for r in ins:
            buf[at : at + r.shape[0], :] = r[...]
            at += r.shape[0]
        for i, (h, p) in enumerate(row_blocks(groups)):
            src = pl.multiple_of((h * groups + (me_ref[0] ^ p)) * step, step)
            out[i * step : (i + 1) * step, :] = buf[pl.ds(src, step), :]

    whole = lambda a: pl.BlockSpec(a.shape, lambda i, m: (0, 0))
    return pl.pallas_call(
        kernel,
        grid_spec=pltpu.PrefetchScalarGridSpec(
            num_scalar_prefetch=1,
            grid=(1,),
            in_specs=[whole(p) for p in parts],
            out_specs=pl.BlockSpec((rows, cols), lambda i, m: (0, 0)),
            scratch_shapes=[pltpu.VMEM((rows, cols), BF16)],
        ),
        out_shape=jax.ShapeDtypeStruct((rows, cols), BF16),
        compiler_params=params(4),
    )(me, *parts)


def fetch(weights, chunks, bn):
    k = weights[0].shape[0]
    shapes = [pltpu.VMEM((k, (last - first) * bn), BF16) for _, first, last in chunks]
    count = len(chunks)

    def kernel(*refs):
        ins, outs, sems = refs[: len(weights)], refs[len(weights) : -1], refs[-1]
        copies = []
        for i, (which, first, last) in enumerate(chunks):
            cols = pl.ds(first * bn, (last - first) * bn)
            copies.append(pltpu.make_async_copy(ins[which].at[:, cols], outs[i], sems.at[i]))
        for c in copies:
            c.start()
        for c in copies:
            c.wait()

    return pl.pallas_call(
        kernel,
        in_specs=[pl.BlockSpec(memory_space=pl.ANY)] * len(weights),
        out_specs=[pl.BlockSpec(memory_space=pltpu.VMEM)] * count,
        out_shape=shapes,
        scratch_shapes=[pltpu.SemaphoreType.DMA((count,))],
        compiler_params=params(1),
        cost_estimate=pl.CostEstimate(flops=0, transcendentals=0, bytes_accessed=4 * weights[0].size),
    )(*weights)


def gate_up(feats, pair, held, first, last, bn):
    rows, k = feats.shape
    half, n = rows // 2, last - first

    def kernel(x, g, u, keep, send):
        cols = pl.ds(pl.multiple_of(pl.program_id(0) * bn, bn), bn)
        for i, w in enumerate((g, u)):
            tile = w[:, cols] if held[i] else w[...]
            part = jnp.dot(x[...], tile, preferred_element_type=F32)
            keep[i] = part[:half]
            send[i] = part[half:].astype(send.dtype)

    o_spec = pl.BlockSpec((2, half, bn), lambda j: (0, 0, j))
    stream = pl.BlockSpec((k, bn), lambda j: (0, first + j))
    return pl.pallas_call(
        kernel,
        grid=(n,),
        in_specs=[pl.BlockSpec((rows, k), lambda j: (0, 0))]
        + [pl.BlockSpec(memory_space=pltpu.VMEM) if h else stream for h in held],
        out_specs=[o_spec, o_spec],
        out_shape=[
            jax.ShapeDtypeStruct((2, half, n * bn), F32),
            jax.ShapeDtypeStruct((2, half, n * bn), F32),
        ],
        compiler_params=params(5 if all(held) else 39),
        cost_estimate=cost(rows, k, 2 * n * bn),
    )(feats, *pair)


def fetch_rows(weight, chunks, bn):
    n = weight.shape[1]
    shapes = [pltpu.VMEM(((last - first) * bn, n), BF16) for first, last in chunks]
    count = len(chunks)

    def kernel(w, *refs):
        outs, sems = refs[:-1], refs[-1]
        copies = []
        for i, (first, last) in enumerate(chunks):
            rows = pl.ds(first * bn, (last - first) * bn)
            copies.append(pltpu.make_async_copy(w.at[rows], outs[i], sems.at[i]))
        for c in copies:
            c.start()
        for c in copies:
            c.wait()

    return pl.pallas_call(
        kernel,
        in_specs=[pl.BlockSpec(memory_space=pl.ANY)],
        out_specs=[pl.BlockSpec(memory_space=pltpu.VMEM)] * count,
        out_shape=shapes,
        scratch_shapes=[pltpu.SemaphoreType.DMA((count,))],
        compiler_params=params(14),
        cost_estimate=pl.CostEstimate(flops=0, transcendentals=0, bytes_accessed=4 * weight.size),
    )(weight)


def down(me, mine, other, acc, held, groups, kinds):
    w = mine.shape[1]
    rows, n = 2 * mine.shape[0], held[0].shape[1]
    step = rows // groups
    bn = block_of(n)
    count = len(held)

    def kernel(me_ref, *refs):
        a, b, wds = refs[0], refs[1], refs[2 : 2 + count]
        outs, lhs = refs[2 + count + (acc is not None) : -1], refs[-1]

        @pl.when(pl.program_id(0) == 0)
        def _():
            for p in range(groups):
                dst = pl.multiple_of((me_ref[0] ^ p) * step, step)
                lhs[pl.ds(dst, step), :] = (a, b)[p % 2][p // 2 * step : (p // 2 + 1) * step, :]

        cols = pl.ds(pl.multiple_of(pl.program_id(0) * bn, bn), bn)
        total = None if acc is None else refs[2 + count][...]
        at = 0
        for wd in wds:
            part = jnp.dot(lhs[:, at : at + wd.shape[0]], wd[:, cols], preferred_element_type=F32)
            total = part if total is None else total + part
            at += wd.shape[0]
        each = rows // len(outs)
        for s, o in enumerate(outs):
            o[...] = total[s * each : (s + 1) * each].astype(o.dtype)

    h_spec = pl.BlockSpec(mine.shape, lambda j, m: (0, 0))
    in_specs = [h_spec, h_spec] + [pl.BlockSpec(memory_space=pltpu.VMEM)] * count
    args = [mine, other, *held]
    if acc is not None:
        in_specs.append(pl.BlockSpec((rows, bn), lambda j, m: (0, j)))
        args.append(acc)
    each = rows // len(kinds)
    return pl.pallas_call(
        kernel,
        grid_spec=pltpu.PrefetchScalarGridSpec(
            num_scalar_prefetch=1,
            grid=(n // bn,),
            in_specs=in_specs,
            out_specs=[pl.BlockSpec((each, bn), lambda j, m: (0, j))] * len(kinds),
            scratch_shapes=[pltpu.VMEM((rows, w), BF16)],
        ),
        out_shape=[jax.ShapeDtypeStruct((each, n), k) for k in kinds],
        compiler_params=params(12),
        cost_estimate=cost(rows, w, n),
    )(me, *args)


def make(nx, nz):
    def swap(v, mask):
        return lax.ppermute(v, "gx", [(i, i ^ mask) for i in range(nx)])

    def across(v, mask):
        return lax.ppermute(v, "gy", [(i, i ^ mask) for i in range(nz)])

    chips = nx // 2
    bits = chips.bit_length() - 1

    def layer(tokens, gate_weight, up_weight, down_weight):
        me = lax.axis_index("gx").astype(jnp.int32).reshape(1)
        parts = [tokens] + [across(tokens, s) for s in range(1, nz)]
        feats = place_rows(me, parts, nx)
        hid = gate_weight.shape[1]
        bn = block_of(hid)
        chunks = widths(hid // bn)
        both = (gate_weight, up_weight)
        early = [(i, *chunks[c]) for c, i in HELD]
        got = fetch(both, early, bn)
        weights = [list(both) for _ in chunks]
        for (c, i), v in zip(HELD, got):
            weights[c][i] = v
        own = feats.shape[0] // (2 * nx)
        hiddens = {}
        for c, (first, last) in enumerate(chunks):
            keep, send = gate_up(feats, weights[c], [(c, i) in HELD for i in range(2)], first, last, bn)
            got = swap(send, 1)
            for h in range(2):
                order = range(bits) if (h + c) % 2 else range(bits)[::-1]
                rows = slice(h * chips * own, (h + 1) * chips * own)
                block = keep[:, rows] + got[:, rows]
                for i, b in enumerate(order):
                    inner = own * 2 ** sum(1 for o in order[i + 1 :] if o < b)
                    wide = block.reshape(2, -1, 2, inner, block.shape[2])
                    stay, go = wide[:, :, 0], wide[:, :, 1].astype(BF16)
                    flat = (2, block.shape[1] // 2, block.shape[2])
                    come = swap(go.reshape(flat), 2 << b)
                    block = stay.reshape(flat) + come.astype(F32)
                hiddens[h, c] = (jax.nn.silu(block[0]) * block[1]).astype(BF16)
        held = fetch_rows(down_weight, chunks, bn)
        outs = {}
        for h in (1, 0):
            acc = None
            for g, group in enumerate(GROUPS[h]):
                hidden = jnp.concatenate([hiddens[h, c] for c in group], axis=1)
                every = [hidden] + [swap(hidden, 2 * q) for q in range(1, chips)]
                mine = jnp.concatenate(every, axis=0)
                other = swap(mine, 1)
                last = g == len(GROUPS[h]) - 1
                kinds = [F32] if not last else [BF16 if h or s else F32 for s in range(nz // 2)]
                acc = down(me, mine, other, acc, [held[c] for c in group], nx, kinds)
                acc = acc if last else acc[0]
            for s in range(nz // 2):
                outs[h * nz // 2 + s] = acc[s]
        total = outs[0]
        for s in list(range(nz // 2, nz)) + list(range(1, nz // 2)):
            come = across(outs[s], s)
            total = total + come.astype(F32)
        return total.astype(BF16)

    return layer


def solution(mesh):
    return jax.shard_map(
        make(mesh.shape["gx"], mesh.shape["gy"]),
        mesh=mesh,
        in_specs=(P("gy", "gx"), P("gx", "gy"), P("gx", "gy"), P("gy", "gx")),
        out_specs=P("gy", "gx"),
        check_vma=False,
    )
```

```python
import jax
import jax.numpy as jnp
from jax import lax
from jax.experimental import pallas as pl
from jax.experimental.pallas import tpu as pltpu
from jax.sharding import PartitionSpec as P

F32 = jnp.float32
BF16 = jnp.bfloat16
PIECES = (4, 5, 4)
GROUPS = (((0, 1, 2),), ((0,), (1, 2)))
HELD = ((0, 0), (0, 1), (1, 0), (1, 1))


def params(mib):
    return pltpu.CompilerParams(vmem_limit_bytes=mib << 20)


def cost(m, k, n):
    return pl.CostEstimate(flops=2 * m * k * n, transcendentals=0, bytes_accessed=2 * (m * k + k * n) + 4 * m * n)


def widths(units):
    total, ends, run = sum(PIECES), [0], 0
    for piece in PIECES:
        run += piece
        ends.append(round(units * run / total))
    return [(a, b) for a, b in zip(ends, ends[1:]) if b > a]


def block_of(size):
    return next(b for b in (512, 256, 128) if size % b == 0)


def row_blocks(groups):
    chips = groups // 2
    return [(h, 2 * q + core) for core in range(2) for h in range(2) for q in range(chips)]


def place_rows(me, parts, groups):
    rows = sum(p.shape[0] for p in parts)
    cols = parts[0].shape[1]
    step = rows // (2 * groups)

    def kernel(me_ref, *refs):
        ins, out, buf = refs[:-2], refs[-2], refs[-1]
        at = 0
        for r in ins:
            buf[at : at + r.shape[0], :] = r[...]
            at += r.shape[0]
        for i, (h, p) in enumerate(row_blocks(groups)):
            src = pl.multiple_of((h * groups + (me_ref[0] ^ p)) * step, step)
            out[i * step : (i + 1) * step, :] = buf[pl.ds(src, step), :]

    whole = lambda a: pl.BlockSpec(a.shape, lambda i, m: (0, 0))
    return pl.pallas_call(
        kernel,
        grid_spec=pltpu.PrefetchScalarGridSpec(
            num_scalar_prefetch=1,
            grid=(1,),
            in_specs=[whole(p) for p in parts],
            out_specs=pl.BlockSpec((rows, cols), lambda i, m: (0, 0)),
            scratch_shapes=[pltpu.VMEM((rows, cols), BF16)],
        ),
        out_shape=jax.ShapeDtypeStruct((rows, cols), BF16),
        compiler_params=params(4),
    )(me, *parts)


def fetch(weights, chunks, bn):
    k = weights[0].shape[0]
    shapes = [pltpu.VMEM((k, (last - first) * bn), BF16) for _, first, last in chunks]
    count = len(chunks)

    def kernel(*refs):
        ins, outs, sems = refs[: len(weights)], refs[len(weights) : -1], refs[-1]
        copies = []
        for i, (which, first, last) in enumerate(chunks):
            cols = pl.ds(first * bn, (last - first) * bn)
            copies.append(pltpu.make_async_copy(ins[which].at[:, cols], outs[i], sems.at[i]))
        for c in copies:
            c.start()
        for c in copies:
            c.wait()

    return pl.pallas_call(
        kernel,
        in_specs=[pl.BlockSpec(memory_space=pl.ANY)] * len(weights),
        out_specs=[pl.BlockSpec(memory_space=pltpu.VMEM)] * count,
        out_shape=shapes,
        scratch_shapes=[pltpu.SemaphoreType.DMA((count,))],
        compiler_params=params(1),
        cost_estimate=pl.CostEstimate(flops=0, transcendentals=0, bytes_accessed=4 * weights[0].size),
    )(*weights)


def gate_up(feats, pair, held, first, last, bn):
    rows, k = feats.shape
    half, n = rows // 2, last - first

    def kernel(x, g, u, keep, send):
        cols = pl.ds(pl.multiple_of(pl.program_id(0) * bn, bn), bn)
        for i, w in enumerate((g, u)):
            tile = w[:, cols]
            part = jnp.dot(x[...], tile, preferred_element_type=F32)
            keep[i] = part[:half]
            send[i] = part[half:].astype(send.dtype)

    def deep(x, g, u, keep, send, buf, sems):
        j = pl.program_id(0)

        def copies(i):
            cols = pl.ds(pl.multiple_of((first + i) * bn, bn), bn)
            return [pltpu.make_async_copy(w.at[:, cols], buf.at[i, q], sems.at[i, q]) for q, w in enumerate((g, u))]

        @pl.when(j == 0)
        def _():
            for i in range(min(3, n)):
                for c in copies(i):
                    c.start()

        for q, c in enumerate(copies(j)):
            c.wait()
            part = jnp.dot(x[...], buf[j, q], preferred_element_type=F32)
            keep[q] = part[:half]
            send[q] = part[half:]

        @pl.when(j + 3 < n)
        def _():
            for c in copies(j + 3):
                c.start()

    o_spec = pl.BlockSpec((2, half, bn), lambda j: (0, 0, j))
    return pl.pallas_call(
        kernel if all(held) else deep,
        grid=(n,),
        in_specs=[pl.BlockSpec((rows, k), lambda j: (0, 0))]
        + [pl.BlockSpec(memory_space=pltpu.VMEM if all(held) else pl.ANY)] * 2,
        scratch_shapes=[] if all(held) else [pltpu.VMEM((n, 2, k, bn), BF16), pltpu.SemaphoreType.DMA((n, 2))],
        out_specs=[o_spec, o_spec],
        out_shape=[
            jax.ShapeDtypeStruct((2, half, n * bn), F32),
            jax.ShapeDtypeStruct((2, half, n * bn), F32),
        ],
        compiler_params=params(5 if all(held) else 39),
        cost_estimate=cost(rows, k, 2 * n * bn),
    )(feats, *pair)


def fetch_rows(weight, chunks, bn):
    n = weight.shape[1]
    shapes = [pltpu.VMEM(((last - first) * bn, n), BF16) for first, last in chunks]
    count = len(chunks)

    def kernel(w, *refs):
        outs, sems = refs[:-1], refs[-1]
        copies = []
        for i, (first, last) in enumerate(chunks):
            rows = pl.ds(first * bn, (last - first) * bn)
            copies.append(pltpu.make_async_copy(w.at[rows], outs[i], sems.at[i]))
        for c in copies:
            c.start()
        for c in copies:
            c.wait()

    return pl.pallas_call(
        kernel,
        in_specs=[pl.BlockSpec(memory_space=pl.ANY)],
        out_specs=[pl.BlockSpec(memory_space=pltpu.VMEM)] * count,
        out_shape=shapes,
        scratch_shapes=[pltpu.SemaphoreType.DMA((count,))],
        compiler_params=params(14),
        cost_estimate=pl.CostEstimate(flops=0, transcendentals=0, bytes_accessed=4 * weight.size),
    )(weight)


def down(me, mine, other, acc, held, groups, kinds):
    w = mine.shape[1]
    rows, n = 2 * mine.shape[0], held[0].shape[1]
    step = rows // groups
    bn = block_of(n)
    count = len(held)

    def kernel(me_ref, *refs):
        a, b, wds = refs[0], refs[1], refs[2 : 2 + count]
        outs, lhs = refs[2 + count + (acc is not None) : -1], refs[-1]

        @pl.when(pl.program_id(0) == 0)
        def _():
            for p in range(groups):
                dst = pl.multiple_of((me_ref[0] ^ p) * step, step)
                lhs[pl.ds(dst, step), :] = (a, b)[p % 2][p // 2 * step : (p // 2 + 1) * step, :]

        cols = pl.ds(pl.multiple_of(pl.program_id(0) * bn, bn), bn)
        total = None if acc is None else refs[2 + count][...]
        at = 0
        for wd in wds:
            part = jnp.dot(lhs[:, at : at + wd.shape[0]], wd[:, cols], preferred_element_type=F32)
            total = part if total is None else total + part
            at += wd.shape[0]
        each = rows // len(outs)
        for s, o in enumerate(outs):
            o[...] = total[s * each : (s + 1) * each].astype(o.dtype)

    h_spec = pl.BlockSpec(mine.shape, lambda j, m: (0, 0))
    in_specs = [h_spec, h_spec] + [pl.BlockSpec(memory_space=pltpu.VMEM)] * count
    args = [mine, other, *held]
    if acc is not None:
        in_specs.append(pl.BlockSpec((rows, bn), lambda j, m: (0, j)))
        args.append(acc)
    each = rows // len(kinds)
    return pl.pallas_call(
        kernel,
        grid_spec=pltpu.PrefetchScalarGridSpec(
            num_scalar_prefetch=1,
            grid=(n // bn,),
            in_specs=in_specs,
            out_specs=[pl.BlockSpec((each, bn), lambda j, m: (0, j))] * len(kinds),
            scratch_shapes=[pltpu.VMEM((rows, w), BF16)],
        ),
        out_shape=[jax.ShapeDtypeStruct((each, n), k) for k in kinds],
        compiler_params=params(12),
        cost_estimate=cost(rows, w, n),
    )(me, *args)


def make(nx, nz):
    def swap(v, mask):
        return lax.ppermute(v, "gx", [(i, i ^ mask) for i in range(nx)])

    def across(v, mask):
        return lax.ppermute(v, "gy", [(i, i ^ mask) for i in range(nz)])

    chips = nx // 2
    bits = chips.bit_length() - 1

    def layer(tokens, gate_weight, up_weight, down_weight):
        me = lax.axis_index("gx").astype(jnp.int32).reshape(1)
        parts = [tokens] + [across(tokens, s) for s in range(1, nz)]
        feats = place_rows(me, parts, nx)
        hid = gate_weight.shape[1]
        bn = block_of(hid)
        chunks = widths(hid // bn)
        both = (gate_weight, up_weight)
        early = [(i, *chunks[c]) for c, i in HELD]
        got = fetch(both, early, bn)
        weights = [list(both) for _ in chunks]
        for (c, i), v in zip(HELD, got):
            weights[c][i] = v
        own = feats.shape[0] // (2 * nx)
        hiddens = {}
        for c, (first, last) in enumerate(chunks):
            keep, send = gate_up(feats, weights[c], [(c, i) in HELD for i in range(2)], first, last, bn)
            got = swap(send, 1)
            for h in range(2):
                order = range(bits) if (h + c) % 2 else range(bits)[::-1]
                rows = slice(h * chips * own, (h + 1) * chips * own)
                block = keep[:, rows] + got[:, rows]
                for i, b in enumerate(order):
                    inner = own * 2 ** sum(1 for o in order[i + 1 :] if o < b)
                    wide = block.reshape(2, -1, 2, inner, block.shape[2])
                    stay, go = wide[:, :, 0], wide[:, :, 1].astype(BF16)
                    flat = (2, block.shape[1] // 2, block.shape[2])
                    come = swap(go.reshape(flat), 2 << b)
                    block = stay.reshape(flat) + come.astype(F32)
                hiddens[h, c] = (jax.nn.silu(block[0]) * block[1]).astype(BF16)
        held = fetch_rows(down_weight, chunks, bn)
        outs = {}
        for h in (1, 0):
            acc = None
            for g, group in enumerate(GROUPS[h]):
                hidden = jnp.concatenate([hiddens[h, c] for c in group], axis=1)
                every = [hidden] + [swap(hidden, 2 * q) for q in range(1, chips)]
                mine = jnp.concatenate(every, axis=0)
                other = swap(mine, 1)
                last = g == len(GROUPS[h]) - 1
                kinds = [F32] if not last else [BF16 if h or s else F32 for s in range(nz // 2)]
                acc = down(me, mine, other, acc, [held[c] for c in group], nx, kinds)
                acc = acc if last else acc[0]
            for s in range(nz // 2):
                outs[h * nz // 2 + s] = acc[s]
        total = outs[0]
        for s in list(range(nz // 2, nz)) + list(range(1, nz // 2)):
            come = across(outs[s], s)
            total = total + come.astype(F32)
        return total.astype(BF16)

    return layer


def solution(mesh):
    return jax.shard_map(
        make(mesh.shape["gx"], mesh.shape["gy"]),
        mesh=mesh,
        in_specs=(P("gy", "gx"), P("gx", "gy"), P("gx", "gy"), P("gy", "gx")),
        out_specs=P("gy", "gx"),
        check_vma=False,
    )
```

```python
import jax
import jax.numpy as jnp
from jax import lax
from jax.experimental import pallas as pl
from jax.experimental.pallas import tpu as pltpu
from jax.sharding import PartitionSpec as P

F32 = jnp.float32
BF16 = jnp.bfloat16
PIECES = (4, 5, 4)
GROUPS = (((0, 1, 2),), ((0,), (1, 2)))
HELD = ((0, 0), (0, 1), (1, 0), (1, 1))


def params(mib):
    return pltpu.CompilerParams(vmem_limit_bytes=mib << 20)


def cost(m, k, n):
    return pl.CostEstimate(flops=2 * m * k * n, transcendentals=0, bytes_accessed=2 * (m * k + k * n) + 4 * m * n)


def widths(units):
    total, ends, run = sum(PIECES), [0], 0
    for piece in PIECES:
        run += piece
        ends.append(round(units * run / total))
    return [(a, b) for a, b in zip(ends, ends[1:]) if b > a]


def block_of(size):
    return next(b for b in (512, 256, 128) if size % b == 0)


def row_blocks(groups):
    chips = groups // 2
    return [(h, 2 * q + core) for core in range(2) for h in range(2) for q in range(chips)]


def place_rows(me, parts, groups):
    rows = sum(p.shape[0] for p in parts)
    cols = parts[0].shape[1]
    step = rows // (2 * groups)

    def kernel(me_ref, *refs):
        ins, out, buf = refs[:-2], refs[-2], refs[-1]
        at = 0
        for r in ins:
            buf[at : at + r.shape[0], :] = r[...]
            at += r.shape[0]
        for i, (h, p) in enumerate(row_blocks(groups)):
            src = pl.multiple_of((h * groups + (me_ref[0] ^ p)) * step, step)
            out[i * step : (i + 1) * step, :] = buf[pl.ds(src, step), :]

    whole = lambda a: pl.BlockSpec(a.shape, lambda i, m: (0, 0))
    return pl.pallas_call(
        kernel,
        grid_spec=pltpu.PrefetchScalarGridSpec(
            num_scalar_prefetch=1,
            grid=(1,),
            in_specs=[whole(p) for p in parts],
            out_specs=pl.BlockSpec((rows, cols), lambda i, m: (0, 0)),
            scratch_shapes=[pltpu.VMEM((rows, cols), BF16)],
        ),
        out_shape=jax.ShapeDtypeStruct((rows, cols), BF16),
        compiler_params=params(4),
    )(me, *parts)


def fetch(weights, chunks, bn):
    k = weights[0].shape[0]
    shapes = [pltpu.VMEM((k, (last - first) * bn), BF16) for _, first, last in chunks]
    count = len(chunks)

    def kernel(*refs):
        ins, outs, sems = refs[: len(weights)], refs[len(weights) : -1], refs[-1]
        copies = []
        for i, (which, first, last) in enumerate(chunks):
            cols = pl.ds(first * bn, (last - first) * bn)
            copies.append(pltpu.make_async_copy(ins[which].at[:, cols], outs[i], sems.at[i]))
        for c in copies:
            c.start()
        for c in copies:
            c.wait()

    return pl.pallas_call(
        kernel,
        in_specs=[pl.BlockSpec(memory_space=pl.ANY)] * len(weights),
        out_specs=[pl.BlockSpec(memory_space=pltpu.VMEM)] * count,
        out_shape=shapes,
        scratch_shapes=[pltpu.SemaphoreType.DMA((count,))],
        compiler_params=params(1),
        cost_estimate=pl.CostEstimate(flops=0, transcendentals=0, bytes_accessed=4 * weights[0].size),
    )(*weights)


def gate_up(feats, pair, held, first, last, bn):
    rows, k = feats.shape
    half, n = rows // 2, last - first

    def kernel(x, g, u, keep, send):
        cols = pl.ds(pl.multiple_of(pl.program_id(0) * bn, bn), bn)
        for i, w in enumerate((g, u)):
            tile = w[:, cols]
            part = jnp.dot(x[...], tile, preferred_element_type=F32)
            keep[i] = part[:half]
            send[i] = part[half:].astype(send.dtype)

    def deep(x, g, u, keep, send, buf, sems):
        j = pl.program_id(0)

        def copies(i):
            cols = pl.ds(pl.multiple_of((first + i) * bn, bn), bn)
            return [pltpu.make_async_copy(w.at[:, cols], buf.at[i, q], sems.at[i, q]) for q, w in enumerate((g, u))]

        @pl.when(j == 0)
        def _():
            for i in range(min(4, n)):
                for c in copies(i):
                    c.start()

        for q, c in enumerate(copies(j)):
            c.wait()
            part = jnp.dot(x[...], buf[j, q], preferred_element_type=F32)
            keep[q] = part[:half]
            send[q] = part[half:]

        @pl.when(j + 4 < n)
        def _():
            for c in copies(j + 4):
                c.start()

    o_spec = pl.BlockSpec((2, half, bn), lambda j: (0, 0, j))
    return pl.pallas_call(
        kernel if all(held) else deep,
        grid=(n,),
        in_specs=[pl.BlockSpec((rows, k), lambda j: (0, 0))]
        + [pl.BlockSpec(memory_space=pltpu.VMEM if all(held) else pl.ANY)] * 2,
        scratch_shapes=[] if all(held) else [pltpu.VMEM((n, 2, k, bn), BF16), pltpu.SemaphoreType.DMA((n, 2))],
        out_specs=[o_spec, o_spec],
        out_shape=[
            jax.ShapeDtypeStruct((2, half, n * bn), F32),
            jax.ShapeDtypeStruct((2, half, n * bn), F32),
        ],
        compiler_params=params(5 if all(held) else 39),
        cost_estimate=cost(rows, k, 2 * n * bn),
    )(feats, *pair)


def fetch_rows(weight, chunks, bn):
    n = weight.shape[1]
    shapes = [pltpu.VMEM(((last - first) * bn, n), BF16) for first, last in chunks]
    count = len(chunks)

    def kernel(w, *refs):
        outs, sems = refs[:-1], refs[-1]
        copies = []
        for i, (first, last) in enumerate(chunks):
            rows = pl.ds(first * bn, (last - first) * bn)
            copies.append(pltpu.make_async_copy(w.at[rows], outs[i], sems.at[i]))
        for c in copies:
            c.start()
        for c in copies:
            c.wait()

    return pl.pallas_call(
        kernel,
        in_specs=[pl.BlockSpec(memory_space=pl.ANY)],
        out_specs=[pl.BlockSpec(memory_space=pltpu.VMEM)] * count,
        out_shape=shapes,
        scratch_shapes=[pltpu.SemaphoreType.DMA((count,))],
        compiler_params=params(14),
        cost_estimate=pl.CostEstimate(flops=0, transcendentals=0, bytes_accessed=4 * weight.size),
    )(weight)


def down(me, mine, other, acc, held, groups, kinds):
    w = mine.shape[1]
    rows, n = 2 * mine.shape[0], held[0].shape[1]
    step = rows // groups
    bn = block_of(n)
    count = len(held)

    def kernel(me_ref, *refs):
        a, b, wds = refs[0], refs[1], refs[2 : 2 + count]
        outs, lhs = refs[2 + count + (acc is not None) : -1], refs[-1]

        @pl.when(pl.program_id(0) == 0)
        def _():
            for p in range(groups):
                dst = pl.multiple_of((me_ref[0] ^ p) * step, step)
                lhs[pl.ds(dst, step), :] = (a, b)[p % 2][p // 2 * step : (p // 2 + 1) * step, :]

        cols = pl.ds(pl.multiple_of(pl.program_id(0) * bn, bn), bn)
        total = None if acc is None else refs[2 + count][...]
        at = 0
        for wd in wds:
            part = jnp.dot(lhs[:, at : at + wd.shape[0]], wd[:, cols], preferred_element_type=F32)
            total = part if total is None else total + part
            at += wd.shape[0]
        each = rows // len(outs)
        for s, o in enumerate(outs):
            o[...] = total[s * each : (s + 1) * each].astype(o.dtype)

    h_spec = pl.BlockSpec(mine.shape, lambda j, m: (0, 0))
    in_specs = [h_spec, h_spec] + [pl.BlockSpec(memory_space=pltpu.VMEM)] * count
    args = [mine, other, *held]
    if acc is not None:
        in_specs.append(pl.BlockSpec((rows, bn), lambda j, m: (0, j)))
        args.append(acc)
    each = rows // len(kinds)
    return pl.pallas_call(
        kernel,
        grid_spec=pltpu.PrefetchScalarGridSpec(
            num_scalar_prefetch=1,
            grid=(n // bn,),
            in_specs=in_specs,
            out_specs=[pl.BlockSpec((each, bn), lambda j, m: (0, j))] * len(kinds),
            scratch_shapes=[pltpu.VMEM((rows, w), BF16)],
        ),
        out_shape=[jax.ShapeDtypeStruct((each, n), k) for k in kinds],
        compiler_params=params(12),
        cost_estimate=cost(rows, w, n),
    )(me, *args)


def make(nx, nz):
    def swap(v, mask):
        return lax.ppermute(v, "gx", [(i, i ^ mask) for i in range(nx)])

    def across(v, mask):
        return lax.ppermute(v, "gy", [(i, i ^ mask) for i in range(nz)])

    chips = nx // 2
    bits = chips.bit_length() - 1

    def layer(tokens, gate_weight, up_weight, down_weight):
        me = lax.axis_index("gx").astype(jnp.int32).reshape(1)
        parts = [tokens] + [across(tokens, s) for s in range(1, nz)]
        feats = place_rows(me, parts, nx)
        hid = gate_weight.shape[1]
        bn = block_of(hid)
        chunks = widths(hid // bn)
        both = (gate_weight, up_weight)
        early = [(i, *chunks[c]) for c, i in HELD]
        got = fetch(both, early, bn)
        weights = [list(both) for _ in chunks]
        for (c, i), v in zip(HELD, got):
            weights[c][i] = v
        own = feats.shape[0] // (2 * nx)
        hiddens = {}
        for c, (first, last) in enumerate(chunks):
            keep, send = gate_up(feats, weights[c], [(c, i) in HELD for i in range(2)], first, last, bn)
            got = swap(send, 1)
            for h in range(2):
                order = range(bits) if (h + c) % 2 else range(bits)[::-1]
                rows = slice(h * chips * own, (h + 1) * chips * own)
                block = keep[:, rows] + got[:, rows]
                for i, b in enumerate(order):
                    inner = own * 2 ** sum(1 for o in order[i + 1 :] if o < b)
                    wide = block.reshape(2, -1, 2, inner, block.shape[2])
                    stay, go = wide[:, :, 0], wide[:, :, 1].astype(BF16)
                    flat = (2, block.shape[1] // 2, block.shape[2])
                    come = swap(go.reshape(flat), 2 << b)
                    block = stay.reshape(flat) + come.astype(F32)
                hiddens[h, c] = (jax.nn.silu(block[0]) * block[1]).astype(BF16)
        held = fetch_rows(down_weight, chunks, bn)
        outs = {}
        for h in (1, 0):
            acc = None
            for g, group in enumerate(GROUPS[h]):
                hidden = jnp.concatenate([hiddens[h, c] for c in group], axis=1)
                every = [hidden] + [swap(hidden, 2 * q) for q in range(1, chips)]
                mine = jnp.concatenate(every, axis=0)
                other = swap(mine, 1)
                last = g == len(GROUPS[h]) - 1
                kinds = [F32] if not last else [BF16 if h or s else F32 for s in range(nz // 2)]
                acc = down(me, mine, other, acc, [held[c] for c in group], nx, kinds)
                acc = acc if last else acc[0]
            for s in range(nz // 2):
                outs[h * nz // 2 + s] = acc[s]
        total = outs[0]
        for s in list(range(nz // 2, nz)) + list(range(1, nz // 2)):
            come = across(outs[s], s)
            total = total + come.astype(F32)
        return total.astype(BF16)

    return layer


def solution(mesh):
    return jax.shard_map(
        make(mesh.shape["gx"], mesh.shape["gy"]),
        mesh=mesh,
        in_specs=(P("gy", "gx"), P("gx", "gy"), P("gx", "gy"), P("gy", "gx")),
        out_specs=P("gy", "gx"),
        check_vma=False,
    )
```
